512 devices in a mesh: rep: 32 (over y, x_lo, core), blk: 16 (over z, x_hi).
Axes of the slice: x: 4 (x_hi: 2, x_lo: 2; x = x_hi * 2 + x_lo), y: 8, z: 8, core: 2. Of those that a mesh axis runs over, the one named last changes fastest.
Arguments:
- green_samples: bfloat16 [2048, 2, 128, 128], P(('rep', 'blk')), may hold values from -0.22265625 to 0.22265625
- exchange_index_order: int32 [64, 128], P('blk'), may hold values from 0 to 127, each once within a row
- frequency_offset: int32 [64], P('blk'), may hold values from 0 to 127
Outputs:
- vertex: float32 [2, 64, 128, 128], P(None, 'blk', 'rep')
The draws below stay inside these ranges and needn't reach their ends.
Inputs may be any that keep to these rules, and one draw needn't show every extreme that they name: Each row of exchange_index_order names every index of 0 to 127 once.
All inputs are finite; a program needn't handle non-finite values.
Results may differ from the reference program's by a relative error of at most 0.0003.
Values may be sent and summed in bfloat16 or wider, within the bound.
A program may use at most 128 MiB of HBM per device.

```python
import jax
import jax.numpy as jnp
from jax import lax

COMBINED_INDEX = 128
Q = 64
MEASURE_COUNT = 2048


def with_ends(result, key, low, largest):
    spot = [jax.random.randint(jax.random.fold_in(key, axis), (), 0, length) for axis, length in enumerate(result.shape)]
    main_axis = result.shape.index(max(result.shape))
    next_to = spot[:main_axis] + [(spot[main_axis] + 1) % result.shape[main_axis]] + spot[main_axis + 1:]
    return result.at[tuple(spot)].set(low).at[tuple(next_to)].set(largest)


def block_levels(key, dims, shards, low, largest):
    loudness = 1.0
    for dim, shards_of in shards:
        draws = jax.random.uniform(jax.random.fold_in(jax.random.fold_in(key, 6), dim), (shards_of,), jnp.float32, low / len(shards), largest / len(shards))
        loudness = loudness * jnp.repeat(jnp.exp(draws), dims[dim] // shards_of).reshape((-1,) + (1,) * (len(dims) - 1 - dim))
    return loudness


def normal_values(rng, dims, spread, most, pieces=(), kind=jnp.bfloat16):
    loudness = block_levels(rng, dims, pieces, -0.22, 0.18) if pieces else 1.0
    drawn = jax.random.normal(rng, dims, jnp.float32) * spread * loudness
    return jnp.minimum(jnp.maximum(drawn, -most), most).astype(kind)


def setup_inputs(seed: int = 0) -> dict:
    splits = jax.random.split(jax.random.key(seed), 4)
    return {
        "green_samples": normal_values(splits[0], (MEASURE_COUNT, 2, COMBINED_INDEX, COMBINED_INDEX), (1.0 / (2 * COMBINED_INDEX * MEASURE_COUNT) ** 0.25), 0.22265625, ((0, 512),)),
        "exchange_index_order": jax.vmap(lambda own: jax.random.permutation(own, COMBINED_INDEX))(jax.random.split(splits[1], Q)).reshape((Q, COMBINED_INDEX)).astype(jnp.int32),
        "frequency_offset": with_ends(jax.random.randint(splits[2], (Q,), 0, COMBINED_INDEX), jax.random.fold_in(splits[2], 1), 0, COMBINED_INDEX - 1).astype(jnp.int32),
    }


def reference(green_samples, exchange_index_order, frequency_offset):
    green_propagator = green_samples.astype(jnp.float32)
    positions = jnp.arange(COMBINED_INDEX, dtype=jnp.int32)

    def one_tile(index_pair):
        perm_row, shift_val = index_pair
        left = jnp.take(green_propagator, perm_row, axis=3)
        rows = (positions + shift_val) % COMBINED_INDEX
        right = jnp.take(green_propagator, rows, axis=2)
        real_part = jnp.einsum("mik,mkj->ij", left[:, 0], right[:, 0]) - jnp.einsum("mik,mkj->ij", left[:, 1], right[:, 1])
        imag_part = jnp.einsum("mik,mkj->ij", left[:, 0], right[:, 1]) + jnp.einsum("mik,mkj->ij", left[:, 1], right[:, 0])
        return jnp.stack([real_part, imag_part])

    tiles = lax.map(one_tile, (exchange_index_order, frequency_offset))
    return jnp.transpose(tiles, (1, 0, 2, 3)).astype(jnp.float32)
```

```python
import functools

import jax
import jax.numpy as jnp
from jax import lax
from jax.experimental import pallas as pl
from jax.experimental.pallas import tpu as pltpu
from jax.sharding import PartitionSpec as P

MESH = pl.DeviceIdType.MESH
N = 128
OWN = 4
TILES = 32
ROWS = 16
CUBE = [(1, 0, 0), (0, 1, 0), (0, 0, 1), (1, 1, 0), (1, 0, 1), (0, 1, 1), (1, 1, 1)]
PEERS = [
    (a, b, c) for c in (4, 2, 6, 0) for b in (4, 2, 6, 0) for a in (2, 0) if a or b or c
]
INDEX_PEERS = [(a, c) for c in (4, 2, 6, 0) for a in (2, 0) if a or c]


def coords():
    rep, blk = lax.axis_index("rep"), lax.axis_index("blk")
    return (blk % 2) * 2 + (rep // 2) % 2, rep // 4, blk // 2, rep % 2


def device(x, y, z, core):
    x, y, z = (x + 8) % 4, (y + 16) % 8, (z + 16) % 8
    return {"rep": (y * 2 + x % 2) * 2 + core, "blk": z * 2 + x // 2}


def remote(src, dst, send, recv, to):
    return pltpu.make_async_remote_copy(
        src_ref=src, dst_ref=dst, send_sem=send, recv_sem=recv, device_id=to, device_id_type=MESH
    )


def kernel(
    green, order, offset, out, held, cols, select, rows, left, right, total, mine, theirs,
    own_sem, send_sem, recv_sem, pass_send, pass_recv, cols_send, cols_recv, sum_send, sum_recv,
):
    x, y, z, core = coords()
    sign = 1 - 2 * core
    partner = device(x, y, z, 1 - core)
    slot = (z // 2) * 2 + x // 2

    own = pltpu.make_async_copy(green, held.at[core, 0], own_sem)
    own.start()

    barrier = pltpu.get_barrier_semaphore()
    count = 0
    for d in CUBE:
        for s in (1, -1):
            pl.semaphore_signal(
                barrier, inc=1, device_id=device(x + s * d[0], y + s * d[1], z + s * d[2], core), device_id_type=MESH
            )
            count += 1
    pl.semaphore_signal(barrier, inc=1, device_id=partner, device_id_type=MESH)
    count += 1
    for d in PEERS:
        pl.semaphore_signal(
            barrier, inc=1, device_id=device(x + d[0], y + d[1], z + d[2], core), device_id_type=MESH
        )
        count += 1

    row = lax.broadcasted_iota(jnp.int32, (8, N), 0)
    lane = lax.broadcasted_iota(jnp.int32, (8, N), 1)
    shift = jnp.zeros((8, N), jnp.int32)
    for i in range(4):
        shift = jnp.where(row == i, offset[i], shift)
    orders = jnp.concatenate([order[...], order[...]], axis=0)
    cols[slot] = jnp.take_along_axis(orders, (lane - shift + N) & (N - 1), axis=1, mode="promise_in_bounds")

    own.wait()
    pl.semaphore_wait(barrier, count)

    col_copies = []
    for i, d in enumerate(INDEX_PEERS):
        copy = remote(
            cols.at[slot], cols.at[slot], cols_send.at[i], cols_recv.at[i], device(x + d[0], y, z + d[1], core)
        )
        copy.start()
        col_copies.append(copy)
    for i, d in enumerate(CUBE):
        remote(
            held.at[core, 0], held.at[core, 1 + i], send_sem.at[1 + i], recv_sem.at[1 + i],
            device(x + sign * d[0], y + sign * d[1], z + sign * d[2], core),
        ).start()

    def arrival(o):
        return remote(held.at[core, 0], held.at[core, o], send_sem.at[o], recv_sem.at[o], partner)

    def passing(o):
        return remote(held.at[core, o], held.at[core, o], pass_send.at[o], pass_recv.at[o], partner)

    passing(0).start()
    total[...] = jnp.zeros_like(total)
    for i, d in enumerate(INDEX_PEERS):
        from_slot = ((z + 16 - d[1]) % 8 // 2) * 2 + (x + 8 - d[0]) % 4 // 2
        remote(cols.at[slot], cols.at[from_slot], cols_send.at[i], cols_recv.at[i], partner).wait_recv()
    place = lax.broadcasted_iota(jnp.int32, (N, N), 0)
    for t in range(TILES):
        wanted = cols[t // 4, t % 4 : t % 4 + 1, :]
        select[:, t * N : (t + 1) * N] = jnp.where(place == wanted, 1.0, 0.0).astype(jnp.bfloat16)

    upper = lax.broadcasted_iota(jnp.int32, (8, N), 0) < 4
    second_half = core == 1

    def class_rows(ref):
        parts = []
        for yh in range(4):
            both = ref[pl.ds(pl.multiple_of(32 * yh + 16 * (y % 2), 16), 16), :].astype(jnp.float32)
            parts.append(jnp.where(x % 2 == 0, both[0:8], both[8:16]))
        pairs = []
        for a, b in ((0, 1), (2, 3)):
            first = jnp.where(second_half, pltpu.roll(parts[a], 4, 0), parts[a])
            second = jnp.where(second_half, parts[b], pltpu.roll(parts[b], 4, 0))
            pairs.append(jnp.where(upper, first, second))
        return jnp.concatenate(pairs, axis=0).astype(jnp.bfloat16)

    def step(o, carry):
        @pl.when(o < 7)
        def _():
            arrival(o + 1).wait_recv()
            passing(o + 1).start()

        remote(held.at[core, 0], held.at[1 - core, o], pass_send.at[o], pass_recv.at[o], partner).wait_recv()
        for h in range(2):
            for m in range(OWN):
                a = h * OWN + m
                gr, gi = held[h, o, m, 0], held[h, o, m, 1]
                right[a * 256 : a * 256 + 128, 0:128] = gr
                right[a * 256 : a * 256 + 128, 128:256] = gi
                right[a * 256 + 128 : a * 256 + 256, 0:128] = -gi
                right[a * 256 + 128 : a * 256 + 256, 128:256] = gr
                for c in range(2):
                    r = (a * 2 + c) * ROWS
                    rows[r : r + ROWS, :] = class_rows(held.at[h, o, m, c])
        for t2 in range(TILES // 2):
            picked = jnp.dot(
                rows[...], select[:, t2 * 256 : (t2 + 1) * 256], preferred_element_type=jnp.float32
            ).astype(jnp.bfloat16)
            for u in range(2):
                t = t2 * 2 + u
                for b in range(4 * OWN):
                    left[t * ROWS : (t + 1) * ROWS, b * N : (b + 1) * N] = picked[
                        b * ROWS : (b + 1) * ROWS, u * N : (u + 1) * N
                    ]
        total[...] += jnp.dot(left[...], right[...], preferred_element_type=jnp.float32)
        return carry

    lax.fori_loop(0, 8, step, 0)

    for group in range(8):
        for ti in range(4):
            t = group * 4 + ti
            for yh in range(4):
                r = t * ROWS + 8 * (yh // 2)
                re, im = total[r : r + 8, 0:N], total[r : r + 8, N : 2 * N]
                if yh % 2:
                    re = pltpu.roll(re, 4, 0)
                else:
                    im = pltpu.roll(im, 4, 0)
                mine[group * 4 + yh, ti] = jnp.where(upper, re, im)

    def address(d):
        return (((z + d[2]) % 8 // 2) * 2 + (x + d[0]) % 4 // 2) * 4 + (y + d[1]) % 8 // 2

    sums = []
    for i, d in enumerate(PEERS):
        copy = remote(
            mine.at[address(d)], theirs.at[i], sum_send.at[i], sum_recv.at[i],
            device(x + d[0], y + d[1], z + d[2], core),
        )
        copy.start()
        sums.append(copy)
    acc = mine[address((0, 0, 0))]
    for i, copy in reversed(list(enumerate(sums))):
        copy.wait_recv()
        acc = acc + theirs[i]
    out[...] = acc

    for copy in sums + col_copies:
        copy.wait_send()

    def drain(o, carry):
        passing(o).wait_send()

        @pl.when(o > 0)
        def _():
            arrival(o).wait_send()

        return carry

    lax.fori_loop(0, 8, drain, 0)


def body(green_samples, exchange_index_order, frequency_offset):
    bf16, f32 = jnp.bfloat16, jnp.float32
    dma = pltpu.SemaphoreType.DMA
    summed = pl.pallas_call(
        kernel,
        out_shape=jax.ShapeDtypeStruct((4, 8, N), f32),
        in_specs=[
            pl.BlockSpec(memory_space=pl.ANY),
            pl.BlockSpec(memory_space=pltpu.VMEM),
            pl.BlockSpec(memory_space=pltpu.SMEM),
        ],
        out_specs=pl.BlockSpec(memory_space=pltpu.VMEM),
        scratch_shapes=[
            pltpu.VMEM((2, 8, OWN, 2, N, N), bf16),
            pltpu.VMEM((8, 8, N), jnp.int32),
            pltpu.VMEM((N, TILES * N), bf16),
            pltpu.VMEM((4 * OWN * ROWS, N), bf16),
            pltpu.VMEM((TILES * ROWS, 4 * OWN * N), bf16),
            pltpu.VMEM((4 * OWN * N, 2 * N), bf16),
            pltpu.VMEM((TILES * ROWS, 2 * N), f32),
            pltpu.VMEM((32, 4, 8, N), f32),
            pltpu.VMEM((31, 4, 8, N), f32),
            dma, dma((8,)), dma((8,)), dma((8,)), dma((8,)), dma((7,)), dma((7,)), dma((31,)), dma((31,)),
        ],
        compiler_params=pltpu.CompilerParams(collective_id=0, has_side_effects=True, vmem_limit_bytes=48 << 20),
        name="vertex",
    )(green_samples, exchange_index_order, frequency_offset)
    return summed.reshape(4, 2, 4, N).transpose(1, 0, 2, 3)


def solution(mesh):
    placed = (P(("rep", "blk"), None, None, None), P("blk", None), P("blk"))
    return jax.shard_map(
        body, mesh=mesh, in_specs=placed, out_specs=P(None, "blk", "rep", None), check_vma=False
    )
```

```python
import jax
import jax.numpy as jnp
from jax import lax
from jax.experimental import pallas as pl
from jax.experimental.pallas import tpu as pltpu
from jax.sharding import PartitionSpec as P

MESH = pl.DeviceIdType.MESH
N = 128
OWN = 4
CHUNK = 2 * OWN
ROWS = 16
CORNERS = [(), (0,), (1,), (2,), (0, 1), (0, 2), (1, 2), (0, 1, 2)]
ORDERS = [(0, 1, 2), (1, 2, 0), (2, 0, 1), (0, 1, 2), (1, 2, 0)]
PIECES = range(len(ORDERS))


def corner(*axes):
    return CORNERS.index(tuple(sorted(axes)))


def coords():
    rep, blk = lax.axis_index("rep"), lax.axis_index("blk")
    return (blk % 2) * 2 + (rep // 2) % 2, rep // 4, blk // 2, rep % 2


def device(x, y, z, core):
    x, y, z = (x + 8) % 4, (y + 16) % 8, (z + 16) % 8
    return {"rep": (y * 2 + x % 2) * 2 + core, "blk": z * 2 + x // 2}


def remote(src, dst, send, recv, to):
    return pltpu.make_async_remote_copy(
        src_ref=src, dst_ref=dst, send_sem=send, recv_sem=recv, device_id=to, device_id_type=MESH
    )


def signal(sem, to):
    pl.semaphore_signal(sem, inc=1, device_id=to, device_id_type=MESH)


def kernel(
    green, order, offset, out,
    held, orders, shifts, cols, select, rows, left, total, mine, theirs,
    own_sem, send_sem, recv_sem, pass_send, pass_recv, cols_send, cols_recv, sum_send, sum_recv, known,
):
    x, y, z, core = coords()
    sign = 1 - 2 * core
    partner = device(x, y, z, 1 - core)
    across = 3 - x

    small = [
        pltpu.make_async_copy(order, orders.at[pl.ds(0, 4)], own_sem.at[2]),
        pltpu.make_async_copy(order, orders.at[pl.ds(4, 4)], own_sem.at[3]),
        pltpu.make_async_copy(offset, shifts, own_sem.at[4]),
    ]
    own = [
        pltpu.make_async_copy(green.at[:, c], held.at[0, core, :, :, pl.ds(c * N, N)], own_sem.at[c])
        for c in range(2)
    ]
    for copy in small + own:
        copy.start()

    barrier = pltpu.get_barrier_semaphore()
    near = [device(x + s, y, z, core) for s in (1, -1)]
    near += [device(x, y + s, z, core) for s in (1, -1)]
    near += [device(x, y, z + s, core) for s in (1, -1)]
    near += [partner, device(across, y, z, core), device(x + 2, y, z, core)]
    for s in (2, -2):
        near += [device(x, y, z + s, core), device(across, y, z + s, core), device(x, y + s, z, core)]
    for to in near:
        signal(barrier, to)

    for copy in small:
        copy.wait()
    row = lax.broadcasted_iota(jnp.int32, (8, N), 0)
    lane = lax.broadcasted_iota(jnp.int32, (8, N), 1)
    shift = jnp.zeros((8, N), jnp.int32)
    for i in range(4):
        shift = jnp.where(row == i, shifts[i], shift)
    cols[0, 0] = jnp.take_along_axis(orders[...], (lane - shift + N) & (N - 1), axis=1, mode="promise_in_bounds")

    for copy in own:
        copy.wait()
    pl.semaphore_wait(barrier, len(near))

    def send_cols(i, src, dst, to):
        return remote(cols.at[src[0], src[1]], cols.at[dst[0], dst[1]], cols_send.at[i], cols_recv.at[i], to)

    col_copies = [
        send_cols(0, (0, 0), (0, 1), device(across, y, z, core)),
        send_cols(1, (0, 0), (3, 0), device(x, y, z + 2, core)),
        send_cols(2, (0, 0), (1, 0), device(x, y, z - 2, core)),
        send_cols(3, (0, 0), (3, 1), device(across, y, z + 2, core)),
        send_cols(4, (0, 0), (1, 1), device(across, y, z - 2, core)),
        send_cols(5, (1, 0), (2, 0), device(x, y, z - 2, core)),
        send_cols(6, (3, 1), (2, 1), device(x, y, z + 2, core)),
    ]
    for copy in col_copies[:5]:
        copy.start()
    onward = [device(x + sign, y, z, core), device(x, y + sign, z, core), device(x, y, z + sign, core)]

    def piece(o, p):
        if p < 3:
            return held.at[o, core, p]
        return held.at[o, core, 3, :, pl.ds((p - 3) * N, N)]

    def hop(p, *ranks):
        axes = [ORDERS[p][r] for r in ranks]
        o = corner(*axes)
        return remote(
            piece(corner(*axes[:-1]), p), piece(o, p), send_sem.at[o, p], recv_sem.at[o, p], onward[axes[-1]]
        )

    for r in range(3):
        for p in PIECES:
            hop(p, r).start()

    def passing(o):
        return remote(held.at[o, core], held.at[o, core], pass_send.at[o], pass_recv.at[o], partner)

    def passed(o):
        remote(held.at[o, core], held.at[o, 1 - core], pass_send.at[o], pass_recv.at[o], partner).wait_recv()

    passing(0).start()
    for s in (2, -2):
        signal(known.at[0], device(x, y + s, z, core))
    total[...] = jnp.zeros_like(total)
    place = lax.broadcasted_iota(jnp.int32, (N, N), 0)
    upper = row < 4
    second_half = core == 1

    def class_rows(o, h, m, c):
        parts = []
        for b in range(4):
            start = pl.multiple_of(32 * ((y // 2 + b) % 4) + 16 * (y % 2), 16)
            both = held[o, h, m, pl.ds(start, 16), c * N : (c + 1) * N].astype(jnp.float32)
            parts.append(jnp.where(x % 2 == 0, both[0:8], both[8:16]))
        pairs = []
        for a, b in ((0, 1), (2, 3)):
            first = jnp.where(second_half, pltpu.roll(parts[a], 4, 0), parts[a])
            second = jnp.where(second_half, parts[b], pltpu.roll(parts[b], 4, 0))
            pairs.append(jnp.where(upper, first, second))
        return jnp.concatenate(pairs, axis=0).astype(jnp.bfloat16)

    def take_rows(o):
        for h in range(2):
            for m in range(OWN):
                for c in range(2):
                    r = ((h * OWN + m) * 2 + c) * ROWS
                    rows[r : r + ROWS, :] = class_rows(o, h, m, c)

    def choose(g):
        for t in range(8):
            wanted = cols[g, t // 4, t % 4 : t % 4 + 1, :]
            select[g, :, t * N : (t + 1) * N] = jnp.where(place == wanted, 1.0, 0.0).astype(jnp.bfloat16)

    def unit(g, o):
        buf = left.at[g % 2]
        for t2 in range(4):
            picked = jnp.dot(
                rows[...], select[g, :, t2 * 256 : (t2 + 1) * 256], preferred_element_type=jnp.float32
            ).astype(jnp.bfloat16)
            for u in range(2):
                t = t2 * 2 + u
                for a in range(CHUNK):
                    for c in range(2):
                        r = (a * 2 + c) * ROWS
                        buf[c * N + t * ROWS : c * N + (t + 1) * ROWS, a * N : (a + 1) * N] = picked[
                            r : r + ROWS, u * N : (u + 1) * N
                        ]
        total[g] += jnp.dot(
            buf[...], held[o].reshape(CHUNK * N, 2 * N), preferred_element_type=jnp.float32
        )

    passed(0)
    take_rows(0)
    col_copies[0].wait_recv()
    choose(0)
    unit(0, 0)
    for p in PIECES:
        hop(p, 0).wait_recv()
        hop(p, 0, 1).start()
        hop(p, 0, 2).start()
    col_copies[2].wait_recv()
    col_copies[5].start()
    col_copies[3].wait_recv()
    col_copies[6].start()
    col_copies[1].wait_recv()
    col_copies[4].wait_recv()
    choose(1)
    unit(1, 0)
    for p in PIECES:
        hop(p, 1).wait_recv()
        hop(p, 1, 2).start()
    choose(3)
    unit(3, 0)
    for p in PIECES:
        hop(p, 2).wait_recv()
    for o in (1, 2, 3):
        passing(o).start()
    pl.semaphore_wait(known.at[0], 2)
    signal(known.at[1], device(x + 2, y, z, core))
    col_copies[5].wait_recv()
    col_copies[6].wait_recv()
    choose(2)
    unit(2, 0)
    for p in PIECES:
        hop(p, 0, 1).wait_recv()
        hop(p, 0, 1, 2).start()

    def step(o, carry):
        passed(o)
        take_rows(o)
        for g in range(4):
            unit(g, o)

        @pl.when(o == 1)
        def _():
            for p in PIECES:
                hop(p, 0, 2).wait_recv()
                hop(p, 1, 2).wait_recv()
            for i in (4, 5, 6):
                passing(i).start()

        @pl.when(o == 3)
        def _():
            for p in PIECES:
                hop(p, 0, 1, 2).wait_recv()
            passing(7).start()

        @pl.when(o == 2)
        def _():
            pl.semaphore_wait(known.at[1], 1)
            for s in (2, -2):
                signal(known.at[2], device(x, y, z + s, core))

        @pl.when(o == 4)
        def _():
            pl.semaphore_wait(known.at[2], 2)
            for s in (2, -2):
                signal(known.at[3], device(x, y, z + s, core))

        return carry

    lax.fori_loop(1, 7, step, 0)

    passed(7)
    take_rows(7)
    pl.semaphore_wait(known.at[3], 2)
    sums = []
    for g in (2, 1, 3, 0):
        unit(g, 7)
        for e in range(2):
            for ti in range(4):
                for half in range(2):
                    r = (e * 4 + ti) * ROWS + 8 * half
                    re = total[g, r : r + 8, 0:N] - total[g, N + r : N + r + 8, N : 2 * N]
                    im = total[g, r : r + 8, N : 2 * N] + total[g, N + r : N + r + 8, 0:N]
                    mine[g, e, 2 * half, ti] = jnp.where(upper, re, pltpu.roll(im, 4, 0))
                    mine[g, e, 2 * half + 1, ti] = jnp.where(upper, pltpu.roll(re, 4, 0), im)
            for b in (2, 1, 3, 0):
                if g or e or b:
                    copy = remote(
                        mine.at[g, e, b], theirs.at[g, e, b], sum_send.at[g, e, b], sum_recv.at[g, e, b],
                        device(x + 2 * e, y + 2 * b, z + 2 * g, core),
                    )
                    copy.start()
                    sums.append(((g, e, b), copy))
    acc = mine[0, 0, 0]
    for place_of, copy in reversed(sums):
        copy.wait_recv()
        acc = acc + theirs[place_of]
    out[...] = acc

    for _, copy in sums:
        copy.wait_send()
    for copy in col_copies:
        copy.wait_send()

    for o in range(8):
        passing(o).wait_send()
    for p in PIECES:
        for ranks in ((0,), (1,), (2,), (0, 1), (0, 2), (1, 2), (0, 1, 2)):
            hop(p, *ranks).wait_send()


def body(green_samples, exchange_index_order, frequency_offset):
    bf16, f32, i32 = jnp.bfloat16, jnp.float32, jnp.int32
    dma, regular = pltpu.SemaphoreType.DMA, pltpu.SemaphoreType.REGULAR
    summed = pl.pallas_call(
        kernel,
        out_shape=jax.ShapeDtypeStruct((4, 8, N), f32),
        in_specs=[pl.BlockSpec(memory_space=pltpu.HBM)] * 3,
        out_specs=pl.BlockSpec(memory_space=pltpu.VMEM),
        scratch_shapes=[
            pltpu.VMEM((8, 2, OWN, N, 2 * N), bf16),
            pltpu.VMEM((8, N), i32),
            pltpu.SMEM((4,), i32),
            pltpu.VMEM((4, 2, 8, N), i32),
            pltpu.VMEM((4, N, 8 * N), bf16),
            pltpu.VMEM((CHUNK * 2 * ROWS, N), bf16),
            pltpu.VMEM((2, 2 * N, CHUNK * N), bf16),
            pltpu.VMEM((4, 2 * N, 2 * N), f32),
            pltpu.VMEM((4, 2, 4, 4, 8, N), f32),
            pltpu.VMEM((4, 2, 4, 4, 8, N), f32),
            dma((5,)), dma((8, 5)), dma((8, 5)), dma((8,)), dma((8,)), dma((7,)), dma((7,)),
            dma((4, 2, 4)), dma((4, 2, 4)), regular((4,)),
        ],
        compiler_params=pltpu.CompilerParams(collective_id=0, has_side_effects=True, vmem_limit_bytes=67043328),
        name="vertex",
    )(green_samples, exchange_index_order, frequency_offset)
    return summed.reshape(4, 2, 4, N).transpose(1, 0, 2, 3)


def solution(mesh):
    placed = (P(("rep", "blk"), None, None, None), P("blk", None), P("blk"))
    return jax.shard_map(
        body, mesh=mesh, in_specs=placed, out_specs=P(None, "blk", "rep", None), check_vma=False
    )
```

```python
import jax
import jax.numpy as jnp
from jax import lax
from jax.experimental import pallas as pl
from jax.experimental.pallas import tpu as pltpu
from jax.sharding import PartitionSpec as P

MESH = pl.DeviceIdType.MESH
N = 128
OWN = 4
CHUNK = 2 * OWN
ROWS = 16
LEVELS = 32766.0
CORNERS = [(), (0,), (1,), (2,), (0, 1), (0, 2), (1, 2), (0, 1, 2)]
ORDERS = [(0, 1, 2), (1, 2, 0), (2, 0, 1), (0, 1, 2), (1, 2, 0)]
PIECES = range(len(ORDERS))


def corner(*axes):
    return CORNERS.index(tuple(sorted(axes)))


def coords():
    rep, blk = lax.axis_index("rep"), lax.axis_index("blk")
    return (blk % 2) * 2 + (rep // 2) % 2, rep // 4, blk // 2, rep % 2


def device(x, y, z, core):
    x, y, z = (x + 8) % 4, (y + 16) % 8, (z + 16) % 8
    return {"rep": (y * 2 + x % 2) * 2 + core, "blk": z * 2 + x // 2}


def remote(src, dst, send, recv, to):
    return pltpu.make_async_remote_copy(
        src_ref=src, dst_ref=dst, send_sem=send, recv_sem=recv, device_id=to, device_id_type=MESH
    )


def signal(sem, to):
    pl.semaphore_signal(sem, inc=1, device_id=to, device_id_type=MESH)


def pack(parts, ref, at):
    most = jnp.maximum(
        jnp.maximum(jnp.abs(parts[0]), jnp.abs(parts[1])), jnp.maximum(jnp.abs(parts[2]), jnp.abs(parts[3]))
    )
    most = jnp.max(most, axis=0, keepdims=True)
    power = jnp.clip(jnp.ceil(jnp.log2(most) + 1e-3), -111.0, 110.0)
    fit = jnp.exp2(-power) * LEVELS
    whole = [jnp.floor(v * fit + 0.5).astype(jnp.int32) for v in parts]
    for i in range(2):
        ref[(*at, slice(8 * i, 8 * i + 8))] = jnp.bitwise_or(
            jnp.left_shift(whole[2 * i], 16), jnp.bitwise_and(whole[2 * i + 1], 0xFFFF)
        )
    ref[(*at, slice(16, 17))] = power.astype(jnp.int32)


def unpack(ref, at):
    step = jnp.exp2(ref[(*at, slice(16, 17))].astype(jnp.float32)) * (1.0 / LEVELS)
    parts = []
    for i in range(2):
        words = ref[(*at, slice(8 * i, 8 * i + 8))]
        for whole in (jnp.right_shift(words, 16), jnp.right_shift(jnp.left_shift(words, 16), 16)):
            parts.append(whole.astype(jnp.float32) * step)
    return parts


def kernel(
    green, order, offset, out,
    held, orders, shifts, cols, select, rows, left, total, mine, theirs,
    own_sem, send_sem, recv_sem, pass_send, pass_recv, cols_send, cols_recv, sum_send, sum_recv, known,
):
    x, y, z, core = coords()
    sign = 1 - 2 * core
    partner = device(x, y, z, 1 - core)
    across = 3 - x

    small = [
        pltpu.make_async_copy(order, orders.at[pl.ds(0, 4)], own_sem.at[2]),
        pltpu.make_async_copy(order, orders.at[pl.ds(4, 4)], own_sem.at[3]),
        pltpu.make_async_copy(offset, shifts, own_sem.at[4]),
    ]
    own = [
        pltpu.make_async_copy(green.at[:, c], held.at[0, core, :, :, pl.ds(c * N, N)], own_sem.at[c])
        for c in range(2)
    ]
    for copy in small + own:
        copy.start()

    barrier = pltpu.get_barrier_semaphore()
    near = [device(x + s, y, z, core) for s in (1, -1)]
    near += [device(x, y + s, z, core) for s in (1, -1)]
    near += [device(x, y, z + s, core) for s in (1, -1)]
    around = list(near)
    near += [partner]
    for to in near:
        signal(barrier, to)

    for copy in small:
        copy.wait()
    row = lax.broadcasted_iota(jnp.int32, (8, N), 0)
    lane = lax.broadcasted_iota(jnp.int32, (8, N), 1)
    shift = jnp.zeros((8, N), jnp.int32)
    for i in range(4):
        shift = jnp.where(row == i, shifts[i], shift)
    cols[0, 0] = jnp.take_along_axis(orders[...], (lane - shift + N) & (N - 1), axis=1, mode="promise_in_bounds")

    for copy in own:
        copy.wait()
    pl.semaphore_wait(barrier, len(near))

    def send_cols(i, src, dst, to):
        return remote(cols.at[src[0], src[1]], cols.at[dst[0], dst[1]], cols_send.at[i], cols_recv.at[i], to)

    col_copies = [
        send_cols(0, (0, 0), (0, 1), device(across, y, z, core)),
        send_cols(1, (0, 0), (3, 0), device(x, y, z + 2, core)),
        send_cols(2, (0, 0), (1, 0), device(x, y, z - 2, core)),
        send_cols(3, (0, 0), (3, 1), device(across, y, z + 2, core)),
        send_cols(4, (0, 0), (1, 1), device(across, y, z - 2, core)),
        send_cols(5, (1, 0), (2, 0), device(x, y, z - 2, core)),
        send_cols(6, (3, 1), (2, 1), device(x, y, z + 2, core)),
    ]
    col_copies[0].start()
    onward = [device(x + sign, y, z, core), device(x, y + sign, z, core), device(x, y, z + sign, core)]

    def piece(o, p, owner=core):
        if p < 3:
            return held.at[o, owner, p]
        return held.at[o, owner, 3, :, pl.ds((p - 3) * N, N)]

    def hop(p, *ranks):
        axes = [ORDERS[p][r] for r in ranks]
        o = corner(*axes)
        return remote(
            piece(corner(*axes[:-1]), p), piece(o, p), send_sem.at[o, p], recv_sem.at[o, p], onward[axes[-1]]
        )

    for r in range(3):
        for p in PIECES:
            hop(p, r).start()

    def passing(o):
        return remote(held.at[o, core], held.at[o, core], pass_send.at[o, 0], pass_recv.at[o, 0], partner)

    def passed(o):
        remote(held.at[o, core], held.at[o, 1 - core], pass_send.at[o, 0], pass_recv.at[o, 0], partner).wait_recv()

    def passing_last(p):
        return remote(piece(7, p), piece(7, p), pass_send.at[7, p], pass_recv.at[7, p], partner)

    passing(0).start()
    for to in around:
        signal(known.at[4], to)
    pl.semaphore_wait(known.at[4], 6)
    for to in around[4:]:
        signal(known.at[5], to)
    for s in (2, -2):
        signal(known.at[0], device(x, y + s, z, core))
    col_copies[1].start()
    col_copies[2].start()
    total[...] = jnp.zeros_like(total)
    place = lax.broadcasted_iota(jnp.int32, (N, N), 0)
    upper = row < 4
    second_half = core == 1

    def class_rows(o, h, m, c):
        parts = []
        for b in range(4):
            start = pl.multiple_of(32 * ((y // 2 + b) % 4) + 16 * (y % 2), 16)
            both = held[o, h, m, pl.ds(start, 16), c * N : (c + 1) * N].astype(jnp.float32)
            parts.append(jnp.where(x % 2 == 0, both[0:8], both[8:16]))
        pairs = []
        for a, b in ((0, 1), (2, 3)):
            first = jnp.where(second_half, pltpu.roll(parts[a], 4, 0), parts[a])
            second = jnp.where(second_half, parts[b], pltpu.roll(parts[b], 4, 0))
            pairs.append(jnp.where(upper, first, second))
        return jnp.concatenate(pairs, axis=0).astype(jnp.bfloat16)

    def take_rows(o):
        for h in range(2):
            for m in range(OWN):
                for c in range(2):
                    r = ((h * OWN + m) * 2 + c) * ROWS
                    rows[o, r : r + ROWS, :] = class_rows(o, h, m, c)

    def choose(g):
        for t in range(8):
            wanted = cols[g, t // 4, t % 4 : t % 4 + 1, :]
            select[g, :, t * N : (t + 1) * N] = jnp.where(place == wanted, 1.0, 0.0).astype(jnp.bfloat16)

    order_of = [(zh + 4 - z // 2) % 4 for zh in (0, 1, 3, 2)]

    def pick(g, o, k):
        for t in range(4, 8):
            wanted = jnp.broadcast_to(cols[g, t // 4, t % 4 : t % 4 + 1, :], (8, N))
            for a in range(CHUNK):
                for c in range(2):
                    r = (a * 2 + c) * ROWS
                    to = k * 2 * N + c * N + t * ROWS
                    halves = [
                        jnp.take_along_axis(rows[o, r + i : r + i + 8, :].astype(jnp.float32), wanted, axis=1, mode="promise_in_bounds")
                        for i in (0, 8)
                    ]
                    left[to : to + ROWS, a * N : (a + 1) * N] = jnp.concatenate(halves, axis=0).astype(jnp.bfloat16)
        for t2 in range(2):
            picked = jnp.dot(
                rows[o], select[g, :, t2 * 256 : (t2 + 1) * 256], preferred_element_type=jnp.float32
            ).astype(jnp.bfloat16)
            for u in range(2):
                t = t2 * 2 + u
                for a in range(CHUNK):
                    for c in range(2):
                        r = (a * 2 + c) * ROWS
                        to = k * 2 * N + c * N + t * ROWS
                        left[to : to + ROWS, a * N : (a + 1) * N] = picked[r : r + ROWS, u * N : (u + 1) * N]

    def multiply(o, first, count, place):
        total[pl.ds(place, count * 2 * N), :] += jnp.dot(
            left[first * 2 * N : (first + count) * 2 * N, :],
            held[o].reshape(CHUNK * N, 2 * N),
            preferred_element_type=jnp.float32,
        )

    def unit(g):
        zh = (z // 2 + g) % 4
        pick(g, 0, g)
        multiply(0, g, 1, pl.multiple_of((zh + zh // 2 - 2 * (zh // 3)) * 2 * N, 2 * N))

    def units(o, first, count):
        for k in range(first, first + count):
            pick(order_of[k], o, k)
        multiply(o, first, count, first * 2 * N)

    pl.semaphore_wait(known.at[5], 2)
    col_copies[3].start()
    col_copies[4].start()
    passed(0)
    take_rows(0)
    col_copies[0].wait_recv()
    choose(0)
    unit(0)
    for p in PIECES:
        hop(p, 0).wait_recv()
        hop(p, 0, 1).start()
        hop(p, 0, 2).start()
    col_copies[2].wait_recv()
    col_copies[5].start()
    for p in PIECES:
        hop(p, 1).wait_recv()
        hop(p, 1, 2).start()
    for p in PIECES:
        hop(p, 2).wait_recv()
    for o in (1, 2, 3):
        passing(o).start()
    col_copies[1].wait_recv()
    col_copies[3].wait_recv()
    col_copies[6].start()
    col_copies[4].wait_recv()
    choose(1)
    unit(1)
    for p in PIECES:
        hop(p, 0, 1).wait_recv()
        hop(p, 0, 1, 2).start()
    choose(3)
    unit(3)
    pl.semaphore_wait(known.at[0], 2)
    signal(known.at[1], device(x + 2, y, z, core))
    col_copies[5].wait_recv()
    col_copies[6].wait_recv()
    choose(2)
    unit(2)

    def settle(o, carry):
        passed(o)
        take_rows(o)
        units(o, 0, 4)

        @pl.when(o == 1)
        def _():
            for p in PIECES:
                hop(p, 0, 2).wait_recv()
                hop(p, 1, 2).wait_recv()
            for i in (4, 5, 6):
                passing(i).start()
            pl.semaphore_wait(known.at[1], 1)
            for s in (2, -2):
                signal(known.at[2], device(x, y, z + s, core))

        return carry

    lax.fori_loop(1, 4, settle, 0)
    pl.semaphore_wait(known.at[2], 2)
    for s in (2, -2):
        signal(known.at[3], device(x, y, z + s, core))

    def first_two(o, carry):
        passed(o)
        take_rows(o)
        units(o, 0, 2)

        @pl.when(o == 5)
        def _():
            for p in PIECES:
                hop(p, 0, 1, 2).wait_recv()
                passing_last(p).start()

        return carry

    lax.fori_loop(4, 7, first_two, 0)
    for p in PIECES:
        far = piece(7, p, 1 - core)
        remote(piece(7, p), far, pass_send.at[7, p], pass_recv.at[7, p], partner).wait_recv()
    take_rows(7)
    pl.semaphore_wait(known.at[3], 2)

    def finish(k):
        g, base = order_of[k], k * 2 * N
        for e in range(2):
            parts = [[], [], [], []]
            for ti in range(4):
                for half in range(2):
                    r = base + (e * 4 + ti) * ROWS + 8 * half
                    re = total[r : r + 8, 0:N] - total[N + r : N + r + 8, N : 2 * N]
                    im = total[r : r + 8, N : 2 * N] + total[N + r : N + r + 8, 0:N]
                    parts[2 * half].append(jnp.where(upper, re, pltpu.roll(im, 4, 0)))
                    parts[2 * half + 1].append(jnp.where(upper, pltpu.roll(re, 4, 0), im))
            for b in (2, 1, 3, 0):
                pack(parts[b], mine, (g, e, b))
                copy = summing(g, e, b)
                if e or b:
                    copy.start()
                else:
                    pl.when(g != 0)(copy.start)

    def summing(g, e, b):
        return remote(
            mine.at[g, e, b], theirs.at[g, e, b], sum_send.at[g, e, b], sum_recv.at[g, e, b],
            device(x + 2 * e, y + 2 * b, z + 2 * g, core),
        )

    units(7, 0, 2)
    finish(0)
    finish(1)

    def last_two(o, carry):
        units(o, 2, 2)
        return carry

    lax.fori_loop(4, 8, last_two, 0)
    finish(2)
    finish(3)
    kept = unpack(mine, (0, 0, 0))
    sums = [(g, e, b) for g in range(4) for e in range(2) for b in range(4)][1:]
    for at in sums:
        summing(*at).wait_recv()
        kept = [k + u for k, u in zip(kept, unpack(theirs, at))]
    for ti in range(4):
        out[ti] = kept[ti]

    for at in sums:
        summing(*at).wait_send()
    for copy in col_copies:
        copy.wait_send()

    for o in range(7):
        passing(o).wait_send()
    for p in PIECES:
        passing_last(p).wait_send()
        for ranks in ((0,), (1,), (2,), (0, 1), (0, 2), (1, 2), (0, 1, 2)):
            hop(p, *ranks).wait_send()


def body(green_samples, exchange_index_order, frequency_offset):
    bf16, f32, i32 = jnp.bfloat16, jnp.float32, jnp.int32
    dma, regular = pltpu.SemaphoreType.DMA, pltpu.SemaphoreType.REGULAR
    summed = pl.pallas_call(
        kernel,
        out_shape=jax.ShapeDtypeStruct((4, 8, N), f32),
        in_specs=[pl.BlockSpec(memory_space=pltpu.HBM)] * 3,
        out_specs=pl.BlockSpec(memory_space=pltpu.VMEM),
        scratch_shapes=[
            pltpu.VMEM((8, 2, OWN, N, 2 * N), bf16),
            pltpu.VMEM((8, N), i32),
            pltpu.SMEM((4,), i32),
            pltpu.VMEM((4, 2, 8, N), i32),
            pltpu.VMEM((4, N, 8 * N), bf16),
            pltpu.VMEM((8, CHUNK * 2 * ROWS, N), bf16),
            pltpu.VMEM((8 * N, CHUNK * N), bf16),
            pltpu.VMEM((8 * N, 2 * N), f32),
            pltpu.VMEM((4, 2, 4, 17, N), i32),
            pltpu.VMEM((4, 2, 4, 17, N), i32),
            dma((5,)), dma((8, 5)), dma((8, 5)), dma((8, 5)), dma((8, 5)), dma((7,)), dma((7,)),
            dma((4, 2, 4)), dma((4, 2, 4)), regular((6,)),
        ],
        compiler_params=pltpu.CompilerParams(collective_id=0, has_side_effects=True, vmem_limit_bytes=67043328),
        name="vertex",
    )(green_samples, exchange_index_order, frequency_offset)
    return summed.reshape(4, 2, 4, N).transpose(1, 0, 2, 3)


def solution(mesh):
    placed = (P(("rep", "blk"), None, None, None), P("blk", None), P("blk"))
    return jax.shard_map(
        body, mesh=mesh, in_specs=placed, out_specs=P(None, "blk", "rep", None), check_vma=False
    )
```

```python
import jax
import jax.numpy as jnp
from jax import lax
from jax.experimental import pallas as pl
from jax.experimental.pallas import tpu as pltpu
from jax.sharding import PartitionSpec as P

MESH = pl.DeviceIdType.MESH
N = 128
OWN = 4
CHUNK = 2 * OWN
ROWS = 16
LEVELS = 32766.0
FIRST = (0, 1, 3, 2)
CORNERS = [(), (0,), (1,), (2,), (0, 1), (0, 2), (1, 2), (0, 1, 2)]
ORDERS = [(0, 1, 2), (1, 2, 0), (2, 0, 1), (0, 1, 2), (1, 2, 0)]
PIECES = range(len(ORDERS))


def corner(*axes):
    return CORNERS.index(tuple(sorted(axes)))


def coords():
    rep, blk = lax.axis_index("rep"), lax.axis_index("blk")
    return (blk % 2) * 2 + (rep // 2) % 2, rep // 4, blk // 2, rep % 2


def device(x, y, z, core):
    x, y, z = (x + 8) % 4, (y + 16) % 8, (z + 16) % 8
    return {"rep": (y * 2 + x % 2) * 2 + core, "blk": z * 2 + x // 2}


def remote(src, dst, send, recv, to):
    return pltpu.make_async_remote_copy(
        src_ref=src, dst_ref=dst, send_sem=send, recv_sem=recv, device_id=to, device_id_type=MESH
    )


def signal(sem, to):
    pl.semaphore_signal(sem, inc=1, device_id=to, device_id_type=MESH)


def pack(parts, ref, at):
    most = jnp.maximum(
        jnp.maximum(jnp.abs(parts[0]), jnp.abs(parts[1])), jnp.maximum(jnp.abs(parts[2]), jnp.abs(parts[3]))
    )
    most = jnp.max(most, axis=0, keepdims=True)
    power = jnp.clip(jnp.ceil(jnp.log2(most) + 1e-3), -111.0, 110.0)
    fit = jnp.exp2(-power) * LEVELS
    whole = [jnp.floor(v * fit + 0.5).astype(jnp.int32) for v in parts]
    for i in range(2):
        ref[(*at, slice(8 * i, 8 * i + 8))] = jnp.bitwise_or(
            jnp.left_shift(whole[2 * i], 16), jnp.bitwise_and(whole[2 * i + 1], 0xFFFF)
        )
    ref[(*at, slice(16, 17))] = power.astype(jnp.int32)


def unpack(ref, at):
    step = jnp.exp2(ref[(*at, slice(16, 17))].astype(jnp.float32)) * (1.0 / LEVELS)
    parts = []
    for i in range(2):
        words = ref[(*at, slice(8 * i, 8 * i + 8))]
        for whole in (jnp.right_shift(words, 16), jnp.right_shift(jnp.left_shift(words, 16), 16)):
            parts.append(whole.astype(jnp.float32) * step)
    return parts


def kernel(
    green, order, offset, out,
    held, orders, shifts, cols, select, rows, left, total, mine, theirs,
    own_sem, send_sem, recv_sem, pass_send, pass_recv, cols_send, cols_recv, sum_send, sum_recv, known,
):
    x, y, z, core = coords()
    sign = 1 - 2 * core
    partner = device(x, y, z, 1 - core)
    across = 3 - x

    small = [
        pltpu.make_async_copy(order, orders.at[pl.ds(0, 4)], own_sem.at[2]),
        pltpu.make_async_copy(order, orders.at[pl.ds(4, 4)], own_sem.at[3]),
        pltpu.make_async_copy(offset, shifts, own_sem.at[4]),
    ]
    own = [
        pltpu.make_async_copy(green.at[:, c], held.at[0, core, :, :, pl.ds(c * N, N)], own_sem.at[c])
        for c in range(2)
    ]
    for copy in small + own:
        copy.start()

    barrier = pltpu.get_barrier_semaphore()
    near = [device(x + s, y, z, core) for s in (1, -1)]
    near += [device(x, y + s, z, core) for s in (1, -1)]
    near += [device(x, y, z + s, core) for s in (1, -1)]
    around = list(near)
    near += [partner]
    for to in near:
        signal(barrier, to)

    for copy in small:
        copy.wait()
    row = lax.broadcasted_iota(jnp.int32, (8, N), 0)
    lane = lax.broadcasted_iota(jnp.int32, (8, N), 1)
    shift = jnp.zeros((8, N), jnp.int32)
    for i in range(4):
        shift = jnp.where(row == i, shifts[i], shift)
    cols[0, 0] = jnp.take_along_axis(orders[...], (lane - shift + N) & (N - 1), axis=1, mode="promise_in_bounds")

    for copy in own:
        copy.wait()
    pl.semaphore_wait(barrier, len(near))

    def send_cols(i, src, dst, to):
        return remote(cols.at[src[0], src[1]], cols.at[dst[0], dst[1]], cols_send.at[i], cols_recv.at[i], to)

    col_copies = [
        send_cols(0, (0, 0), (0, 1), device(across, y, z, core)),
        send_cols(1, (0, 0), (3, 0), device(x, y, z + 2, core)),
        send_cols(2, (0, 0), (1, 0), device(x, y, z - 2, core)),
        send_cols(3, (0, 0), (3, 1), device(across, y, z + 2, core)),
        send_cols(4, (0, 0), (1, 1), device(across, y, z - 2, core)),
        send_cols(5, (1, 0), (2, 0), device(x, y, z - 2, core)),
        send_cols(6, (3, 1), (2, 1), device(x, y, z + 2, core)),
    ]
    col_copies[0].start()
    onward = [device(x + sign, y, z, core), device(x, y + sign, z, core), device(x, y, z + sign, core)]

    def piece(o, p, owner=core):
        if p < 3:
            return held.at[o, owner, p]
        return held.at[o, owner, 3, :, pl.ds((p - 3) * N, N)]

    def hop(p, *ranks):
        axes = [ORDERS[p][r] for r in ranks]
        o = corner(*axes)
        return remote(
            piece(corner(*axes[:-1]), p), piece(o, p), send_sem.at[o, p], recv_sem.at[o, p], onward[axes[-1]]
        )

    for r in range(3):
        for p in PIECES:
            hop(p, r).start()

    def passing(o):
        return remote(held.at[o, core], held.at[o, core], pass_send.at[o, 0], pass_recv.at[o, 0], partner)

    def passed(o):
        remote(held.at[o, core], held.at[o, 1 - core], pass_send.at[o, 0], pass_recv.at[o, 0], partner).wait_recv()

    def passing_last(p):
        return remote(piece(7, p), piece(7, p), pass_send.at[7, p], pass_recv.at[7, p], partner)

    passing(0).start()
    for to in around:
        signal(known.at[4], to)
    pl.semaphore_wait(known.at[4], 6)
    for to in around[4:]:
        signal(known.at[5], to)
    for s in (2, -2):
        signal(known.at[0], device(x, y + s, z, core))
    col_copies[1].start()
    col_copies[2].start()
    total[...] = jnp.zeros_like(total)
    place = lax.broadcasted_iota(jnp.int32, (N, N), 0)
    upper = row < 4
    second_half = core == 1

    def class_rows(o, h, m, c):
        parts = []
        for b in range(4):
            start = pl.multiple_of(32 * b + 16 * (y % 2), 16)
            both = held[o, h, m, pl.ds(start, 16), c * N : (c + 1) * N].astype(jnp.float32)
            parts.append(jnp.where(x % 2 == 0, both[0:8], both[8:16]))
        pairs = []
        for a, b in ((0, 1), (2, 3)):
            first = jnp.where(second_half, pltpu.roll(parts[a], 4, 0), parts[a])
            second = jnp.where(second_half, parts[b], pltpu.roll(parts[b], 4, 0))
            pairs.append(jnp.where(upper, first, second))
        return jnp.concatenate(pairs, axis=0).astype(jnp.bfloat16)

    def take_rows(o):
        for h in range(2):
            for m in range(OWN):
                for c in range(2):
                    r = ((h * OWN + m) * 2 + c) * ROWS
                    rows[o, r : r + ROWS, :] = class_rows(o, h, m, c)

    def choose(g):
        for t in range(8):
            wanted = cols[g, t // 4, t % 4 : t % 4 + 1, :]
            select[g, :, t * N : (t + 1) * N] = jnp.where(place == wanted, 1.0, 0.0).astype(jnp.bfloat16)

    order_of = [(zh + 4 - z // 2) % 4 for zh in FIRST]

    def pick(g, o, k):
        for t in range(4, 8):
            wanted = jnp.broadcast_to(cols[g, t // 4, t % 4 : t % 4 + 1, :], (8, N))
            for a in range(CHUNK):
                for c in range(2):
                    r = (a * 2 + c) * ROWS
                    to = k * 2 * N + c * N + t * ROWS
                    halves = [
                        jnp.take_along_axis(rows[o, r + i : r + i + 8, :].astype(jnp.float32), wanted, axis=1, mode="promise_in_bounds")
                        for i in (0, 8)
                    ]
                    left[to : to + ROWS, a * N : (a + 1) * N] = jnp.concatenate(halves, axis=0).astype(jnp.bfloat16)
        for t2 in range(2):
            picked = jnp.dot(
                rows[o], select[g, :, t2 * 256 : (t2 + 1) * 256], preferred_element_type=jnp.float32
            ).astype(jnp.bfloat16)
            for u in range(2):
                t = t2 * 2 + u
                for a in range(CHUNK):
                    for c in range(2):
                        r = (a * 2 + c) * ROWS
                        to = k * 2 * N + c * N + t * ROWS
                        left[to : to + ROWS, a * N : (a + 1) * N] = picked[r : r + ROWS, u * N : (u + 1) * N]

    def multiply(o, first, count, place):
        total[pl.ds(place, count * 2 * N), :] += jnp.dot(
            left[first * 2 * N : (first + count) * 2 * N, :],
            held[o].reshape(CHUNK * N, 2 * N),
            preferred_element_type=jnp.float32,
        )

    def unit(g):
        zh = (z // 2 + g) % 4
        pick(g, 0, g)
        multiply(0, g, 1, pl.multiple_of((zh + zh // 2 - 2 * (zh // 3)) * 2 * N, 2 * N))

    def units(o, first, count):
        for k in range(first, first + count):
            pick(order_of[k], o, k)
        multiply(o, first, count, first * 2 * N)

    pl.semaphore_wait(known.at[5], 2)
    col_copies[3].start()
    col_copies[4].start()
    passed(0)
    take_rows(0)
    col_copies[0].wait_recv()
    choose(0)
    unit(0)
    for p in PIECES:
        hop(p, 0).wait_recv()
        hop(p, 0, 1).start()
        hop(p, 0, 2).start()
    col_copies[2].wait_recv()
    col_copies[5].start()
    for p in PIECES:
        hop(p, 1).wait_recv()
        hop(p, 1, 2).start()
    for p in PIECES:
        hop(p, 2).wait_recv()
    for o in (1, 2, 3):
        passing(o).start()
    col_copies[1].wait_recv()
    col_copies[3].wait_recv()
    col_copies[6].start()
    col_copies[4].wait_recv()
    choose(1)
    unit(1)
    for p in PIECES:
        hop(p, 0, 1).wait_recv()
        hop(p, 0, 1, 2).start()
    choose(3)
    unit(3)
    pl.semaphore_wait(known.at[0], 2)
    signal(known.at[1], device(x + 2, y, z, core))
    col_copies[5].wait_recv()
    col_copies[6].wait_recv()
    choose(2)
    unit(2)

    def settle(o, carry):
        passed(o)
        take_rows(o)
        units(o, 0, 4)

        @pl.when(o == 1)
        def _():
            for p in PIECES:
                hop(p, 0, 2).wait_recv()
                hop(p, 1, 2).wait_recv()
            for i in (4, 5, 6):
                passing(i).start()
            pl.semaphore_wait(known.at[1], 1)
            for s in (2, -2):
                signal(known.at[2], device(x, y, z + s, core))

        return carry

    lax.fori_loop(1, 4, settle, 0)
    pl.semaphore_wait(known.at[2], 2)
    for s in (2, -2):
        signal(known.at[3], device(x, y, z + s, core))

    def first_two(o, carry):
        passed(o)
        take_rows(o)
        units(o, 0, 2)

        @pl.when(o == 5)
        def _():
            for p in PIECES:
                hop(p, 0, 1, 2).wait_recv()
                passing_last(p).start()

        return carry

    lax.fori_loop(4, 7, first_two, 0)
    for p in PIECES:
        far = piece(7, p, 1 - core)
        remote(piece(7, p), far, pass_send.at[7, p], pass_recv.at[7, p], partner).wait_recv()
    take_rows(7)
    pl.semaphore_wait(known.at[3], 2)

    def finish(k):
        g, base = order_of[k], k * 2 * N
        for yh in FIRST:
            half = yh // 2
            for e in range(2):
                parts = []
                for ti in range(4):
                    r = base + (e * 4 + ti) * ROWS + 8 * half
                    re = total[r : r + 8, 0:N] - total[N + r : N + r + 8, N : 2 * N]
                    im = total[r : r + 8, N : 2 * N] + total[N + r : N + r + 8, 0:N]
                    if yh % 2:
                        parts.append(jnp.where(upper, pltpu.roll(re, 4, 0), im))
                    else:
                        parts.append(jnp.where(upper, re, pltpu.roll(im, 4, 0)))
                b = (yh + 4 - y // 2) % 4
                pack(parts, mine, (g, e, b))
                if e:
                    summing(g, e, b).start()
                else:
                    pl.when(g + b != 0)(summing(g, e, b).start)

    def summing(g, e, b):
        return remote(
            mine.at[g, e, b], theirs.at[g, e, b], sum_send.at[g, e, b], sum_recv.at[g, e, b],
            device(x + 2 * e, y + 2 * b, z + 2 * g, core),
        )

    units(7, 0, 2)
    finish(0)
    finish(1)

    def last_two(o, carry):
        units(o, 2, 2)
        return carry

    lax.fori_loop(4, 8, last_two, 0)
    finish(2)
    finish(3)
    kept = unpack(mine, (0, 0, 0))
    sums = [(g, e, b) for g in (0, 3, 2, 1) for b in (0, 3, 1, 2) for e in range(2)][1:]
    for at in sums:
        summing(*at).wait_recv()
        kept = [k + u for k, u in zip(kept, unpack(theirs, at))]
    for ti in range(4):
        out[ti] = kept[ti]

    for at in sums:
        summing(*at).wait_send()
    for copy in col_copies:
        copy.wait_send()

    for o in range(7):
        passing(o).wait_send()
    for p in PIECES:
        passing_last(p).wait_send()
        for ranks in ((0,), (1,), (2,), (0, 1), (0, 2), (1, 2), (0, 1, 2)):
            hop(p, *ranks).wait_send()


def body(green_samples, exchange_index_order, frequency_offset):
    bf16, f32, i32 = jnp.bfloat16, jnp.float32, jnp.int32
    dma, regular = pltpu.SemaphoreType.DMA, pltpu.SemaphoreType.REGULAR
    summed = pl.pallas_call(
        kernel,
        out_shape=pltpu.VMEM((4, 8, N), f32),
        in_specs=[pl.BlockSpec(memory_space=pltpu.HBM)] * 3,
        out_specs=pl.BlockSpec(memory_space=pltpu.VMEM),
        scratch_shapes=[
            pltpu.VMEM((8, 2, OWN, N, 2 * N), bf16),
            pltpu.VMEM((8, N), i32),
            pltpu.SMEM((4,), i32),
            pltpu.VMEM((4, 2, 8, N), i32),
            pltpu.VMEM((4, N, 8 * N), bf16),
            pltpu.VMEM((8, CHUNK * 2 * ROWS, N), bf16),
            pltpu.VMEM((8 * N, CHUNK * N), bf16),
            pltpu.VMEM((8 * N, 2 * N), f32),
            pltpu.VMEM((4, 2, 4, 17, N), i32),
            pltpu.VMEM((4, 2, 4, 17, N), i32),
            dma((5,)), dma((8, 5)), dma((8, 5)), dma((8, 5)), dma((8, 5)), dma((7,)), dma((7,)),
            dma((4, 2, 4)), dma((4, 2, 4)), regular((6,)),
        ],
        compiler_params=pltpu.CompilerParams(collective_id=0, has_side_effects=True, vmem_limit_bytes=48 << 20),
        name="vertex",
    )(*[pltpu.with_memory_space_constraint(a, pltpu.HBM) for a in (green_samples, exchange_index_order, frequency_offset)])
    return summed.reshape(4, 2, 4, N).transpose(1, 0, 2, 3)


def solution(mesh):
    placed = (P(("rep", "blk"), None, None, None), P("blk", None), P("blk"))
    return jax.shard_map(
        body, mesh=mesh, in_specs=placed, out_specs=P(None, "blk", "rep", None), check_vma=False
    )
```
